256 devices in a mesh: segment: 8 (over y, core), seq: 32 (over z, x).
Axes of the slice: x: 4, y: 4, z: 8, core: 2. Of those that a mesh axis runs over, the one named last changes fastest.
Arguments:
- residual: bfloat16 [8, 4096, 8192], P('segment', 'seq'), may hold values from -6 to 6
- query_rows: bfloat16 [8, 2, 4096, 8192], P('segment', None, 'seq'), may hold values from -8 to 8
- key_rows: bfloat16 [8, 2, 4096, 1024], P('segment', None, 'seq'), may hold values from -6 to 6
- value_rows: bfloat16 [8, 2, 4096, 1024], P('segment', None, 'seq'), may hold values from -8 to 8
- pattern: int32 [8, 2, 8, 32, 8], P('segment'), may hold values from -1 to 31, as said below
Outputs:
- section_out: float32 [8, 4096, 8192], P('segment', 'seq')
The draws below stay inside these ranges and needn't reach their ends.
Inputs may be any that keep to these rules, and one draw needn't show every extreme that they name: `pattern`: in each row (section, layer, key-value head, query block i) slot 0 holds i; the entries that are not -1 are distinct and at most i; for every section, layer and key-value head some row has all 8 slots filled.
All inputs are finite; a program needn't handle non-finite values.
Results may differ from the reference program's by a relative error of at most 0.0035.
Values may be sent and summed in bfloat16 or wider, within the bound.
A program may use at most 128 MiB of HBM per device.

```python
import math
import jax
import jax.numpy as jnp
from jax import lax

HQ = 64
HK = 8
HD = 128
LAYERS = 2
BLOCK = 128
NSEL = 8
D = 8192
TOKENS = 4096
NQB = 32
SEGMENTS = 8


def shared_draw(key):
    base_key = jax.random.fold_in(key, 11)
    key_query, key_keys = jax.random.split(base_key, 2)
    query_shape = (SEGMENTS, LAYERS, TOKENS, HQ * HD)
    key_shape = (SEGMENTS, LAYERS, TOKENS, HK * HD)
    query_vals = jnp.clip(jax.random.normal(key_query, query_shape, jnp.float32), -6.0, 6.0)
    key_vals = jnp.clip(jax.random.normal(key_keys, key_shape, jnp.float32), -6.0, 6.0)
    return (query_vals, key_vals)


def draw_query_rows(key, part):
    return shared_draw(key)[0].astype(jnp.bfloat16)


def draw_key_rows(key, part):
    return shared_draw(key)[1].astype(jnp.bfloat16)


def draw_pattern(key, part):
    extra = NSEL - 3
    row_shape = (SEGMENTS, LAYERS, HK, NQB)
    blocks = jnp.arange(NQB, dtype=jnp.int32)
    query_block = blocks.reshape(1, 1, 1, NQB)
    previous_slot = jnp.where(query_block >= 1, query_block - 1, -1)
    global_slot = jnp.where(query_block >= 2, 0, -1)
    key_score, key_cap, key_count = jax.random.split(key, 3)
    candidate = blocks.reshape(1, 1, 1, 1, NQB)
    raw_bits = jax.random.randint(key_score, row_shape + (NQB,), 0, 1 << 20)
    cand_scores = raw_bits * NQB + candidate
    usable = (candidate >= 1) & (candidate <= query_block[..., None] - 2)
    cand_scores = jnp.where(usable, cand_scores, -1)
    top_scores, picked = lax.top_k(cand_scores, extra)
    ceiling = jax.random.randint(key_cap, (SEGMENTS, LAYERS, HK, 1), 0, extra + 1)
    counts = jax.random.randint(key_count, row_shape, 0, ceiling + 1)
    counts = jnp.where(query_block == NQB - 1, extra, counts)
    slot_rank = jnp.arange(extra, dtype=jnp.int32)
    is_live = (slot_rank < counts[..., None]) & (top_scores >= 0)
    randoms = jnp.where(is_live, picked.astype(jnp.int32), -1)
    own_slot = jnp.broadcast_to(query_block, row_shape)[..., None]
    prev_col = jnp.broadcast_to(previous_slot, row_shape)[..., None]
    glob_col = jnp.broadcast_to(global_slot, row_shape)[..., None]
    return jnp.concatenate([own_slot, prev_col, glob_col, randoms], axis=-1).astype(jnp.int32)


def block_scale(own_key, shape, shards, least, high):
    gain = 1.0
    for axis_at, parts in shards:
        heights = jax.random.uniform(jax.random.fold_in(jax.random.fold_in(own_key, 6), axis_at), (parts,), jnp.float32, least / len(shards), high / len(shards))
        gain = gain * jnp.repeat(jnp.exp(heights), shape[axis_at] // parts).reshape((-1,) + (1,) * (len(shape) - 1 - axis_at))
    return gain


def gaussian(key, shape, width, limit, shards=(), kind=jnp.bfloat16):
    gain = block_scale(key, shape, shards, -0.22, 0.18) if shards else 1.0
    values = jax.random.normal(key, shape, jnp.float32) * width * gain
    return jnp.minimum(jnp.maximum(values, -limit), limit).astype(kind)


def setup_inputs(seed: int = 0) -> dict:
    key_of = jax.random.split(jax.random.key(seed), 6)
    return {
        "residual": gaussian(key_of[0], (SEGMENTS, TOKENS, D), 1.0, 6.0, ((0, 8), (1, 32))),
        "query_rows": draw_query_rows(jax.random.fold_in(key_of[5], 71), 0),
        "key_rows": draw_key_rows(jax.random.fold_in(key_of[5], 71), 0),
        "value_rows": gaussian(key_of[3], (SEGMENTS, LAYERS, TOKENS, HK * HD), 2.0, 8.0, ((0, 8), (2, 32))),
        "pattern": draw_pattern(jax.random.fold_in(key_of[5], 71), 0),
    }


def attend(q_rows, k_rows, v_rows, pattern_rows):
    token_count, head_count, head_dim = q_rows.shape
    block_count = token_count // BLOCK
    key_blocks = k_rows.reshape(block_count, BLOCK, head_dim)
    value_blocks = v_rows.reshape(block_count, BLOCK, head_dim)
    query_blocks = q_rows.reshape(block_count // 4, 4, BLOCK, head_count, head_dim)
    chosen_blocks = pattern_rows.reshape(block_count // 4, 4, NSEL)
    own_blocks = jnp.arange(block_count, dtype=jnp.int32).reshape(block_count // 4, 4)
    scaling = 1.0 / math.sqrt(head_dim)
    causal = jnp.arange(BLOCK)[:, None] >= jnp.arange(BLOCK)[None, :]

    def one_group(operands):
        q_group, chosen_group, own_group = operands
        is_live = chosen_group >= 0
        clamped = jnp.maximum(chosen_group, 0).astype(jnp.int32)
        key_sel = key_blocks[clamped]
        value_sel = value_blocks[clamped]
        scores = jnp.einsum('qthd,qskd->qhtsk', q_group.astype(jnp.float32), key_sel.astype(jnp.float32)) * scaling
        on_diagonal = clamped == own_group[:, None]
        allowed = is_live[:, None, None, :, None] & (jnp.logical_not(on_diagonal)[:, None, None, :, None] | causal[None, None, :, None, :])
        scores = jnp.where(allowed, scores, -1e+30)
        row_max = lax.optimization_barrier(jnp.max(scores, axis=(3, 4), keepdims=True))
        weights = jnp.exp(scores - row_max)
        row_total = lax.optimization_barrier(jnp.sum(weights, axis=(3, 4), keepdims=True))
        probability = (weights / row_total).astype(jnp.bfloat16)
        mixed_rows = jnp.einsum('qhtsk,qskd->qthd', probability.astype(jnp.float32), value_sel.astype(jnp.float32))
        return mixed_rows.astype(jnp.bfloat16)
    gathered_out = lax.map(one_group, (query_blocks, chosen_blocks, own_blocks))
    return gathered_out.reshape(token_count, head_count * head_dim)

def reference(residual, query_rows, key_rows, value_rows, pattern):
    group_size = HQ // HK
    results = []
    for section in range(SEGMENTS):
        previous = (section - 1) % SEGMENTS
        running = residual[previous].astype(jnp.float32)
        layer_total = jnp.zeros((TOKENS, HQ * HD), jnp.float32)
        for layer_no in range(LAYERS):
            q_heads = jnp.moveaxis(query_rows[section, layer_no].reshape(TOKENS, HK, group_size, HD), 1, 0)
            k_heads = jnp.moveaxis(key_rows[section, layer_no].reshape(TOKENS, HK, HD), 1, 0)
            v_heads = jnp.moveaxis(value_rows[section, layer_no].reshape(TOKENS, HK, HD), 1, 0)

            def per_head(operands):
                return attend(operands[0], operands[1], operands[2], operands[3])
            attended = lax.map(per_head, (q_heads, k_heads, v_heads, pattern[section, layer_no]))
            attended = jnp.moveaxis(attended, 0, 1).reshape(TOKENS, HQ * HD)
            layer_total = layer_total + attended.astype(jnp.float32)
        layer_sum = layer_total.astype(jnp.bfloat16)
        results.append(running + layer_sum.astype(jnp.float32))
    return jnp.stack(results)
```

```python
import math

import jax
import jax.numpy as jnp
from jax import lax
from jax.experimental import pallas as pl
from jax.experimental.pallas import tpu as pltpu
from jax.sharding import PartitionSpec as P

HQ = 64
HK = 8
HD = 128
LAYERS = 2
BLOCK = 128
NSEL = 8
NZ = 8
NX = 4
UNITS = 4
GROUP = HQ // HK
WIDE = GROUP * HD
EXP2_SCALE = math.log2(math.e) / math.sqrt(HD)
NEG = -1e30
MESH = pl.DeviceIdType.MESH
LAG = 3

HOPS = {(0, 0): 4, (0, 1): 3, (1, 0): 3, (1, 1): 4}


def ring_order(direction):
    kinds = (0, 1) if direction == 0 else (1, 0)
    left = {(u, t): 0 for u in range(UNITS) for t in kinds}
    place = {}
    order = []
    total = sum(HOPS[t, direction] for t in kinds) * UNITS
    while len(order) < total:
        pick = None
        for lag in range(LAG, 0, -1):
            for u in range(UNITS):
                for t in kinds:
                    step = left[u, t]
                    if step == HOPS[t, direction]:
                        continue
                    if step and len(order) - place[u, t, step - 1] < lag:
                        continue
                    key = (u, step, kinds.index(t))
                    if pick is None or key < pick[0]:
                        pick = (key, (u, t, step))
            if pick:
                break
        u, t, step = pick[1]
        place[u, t, step] = len(order)
        left[u, t] += 1
        order.append((u, t, step))
    return order, place


def body(
    pat_ref, res_ref, q_ref, k_ref, v_ref, sum_ref, car_ref,
    kb0, kb1, kb2, kb3, vb0, vb1, vb2, vb3, qb0, qb1, qb2, qb3, ob0, ob1,
    ksel, vsel, diag, pats,
    kx_send, kx_recv, own_sem, z_send, z_recv, q_send, q_recv, o_send, o_recv, o_own,
    pat_sem, car_send, car_recv,
):
    kv = ((kb0, kb1, kb2, kb3), (vb0, vb1, vb2, vb3))
    kv_in = (k_ref, v_ref)
    qb = (qb0, qb1, qb2, qb3)
    ob = (ob0, ob1)
    seg = lax.axis_index("segment")
    me = lax.axis_index("seq")
    z = me // NX
    x = lax.rem(me, NX)
    nseg = lax.axis_size("segment")

    def at_x(d):
        return (seg, z * NX + lax.rem(x + d, NX))

    def at_z(d):
        return (seg, lax.rem(z + d + NZ, NZ) * NX + x)

    after = (lax.rem(seg + 1, nseg), me)
    before = (lax.rem(seg + nseg - 1, nseg), me)

    def pat_copy(u):
        return pltpu.make_async_copy(
            pat_ref.at[0, u % 2, 2 * x + u // 2], pats.at[u], pat_sem.at[u]
        )

    def kv_src(u, t, who):
        cols = pl.multiple_of((2 * who + u // 2) * HD, HD)
        return kv_in[t].at[0, u % 2, :, pl.ds(cols, HD)]

    def q_src(u, who):
        cols = pl.multiple_of((2 * who + u // 2) * WIDE, WIDE)
        return q_ref.at[0, u % 2, :, pl.ds(cols, WIDE)]

    def own_copy(u, t):
        return pltpu.make_async_copy(
            kv_src(u, t, x), kv[t][u].at[z * NX + x], own_sem.at[u, t]
        )

    def own_q(u):
        return pltpu.make_async_copy(q_src(u, x), qb[u].at[x], q_recv.at[u, NX - 1])

    barrier = pltpu.get_barrier_semaphore()
    peers = [at_x(1), at_x(2), at_x(3), at_z(1), at_z(-1), after, before]
    for peer in peers:
        pl.semaphore_signal(barrier, inc=1, device_id=peer, device_id_type=MESH)
    for u in range(UNITS):
        for t in (0, 1):
            own_copy(u, t).start()
    for u in range(UNITS):
        pat_copy(u).start()
        own_q(u).start()
    row = lax.broadcasted_iota(jnp.int32, (BLOCK, BLOCK), 0)
    col = lax.broadcasted_iota(jnp.int32, (BLOCK, BLOCK), 1)
    diag[...] = jnp.where(row >= col, 0.0, NEG).astype(jnp.float32)
    vsel[:, pl.ds(HD, HD)] = jnp.ones((NSEL * BLOCK, HD), jnp.bfloat16)
    pl.semaphore_wait(barrier, len(peers))

    def kx_copy(u, t, d):
        to = lax.rem(x + d, NX)
        return pltpu.make_async_remote_copy(
            src_ref=kv_src(u, t, to),
            dst_ref=kv[t][u].at[z * NX + x],
            send_sem=kx_send.at[u, t, d - 1],
            recv_sem=kx_recv.at[u, t, d - 1],
            device_id=at_x(d),
            device_id_type=MESH,
        )

    def kx_arrived(u, t, d):
        frm = lax.rem(x + NX - d, NX)
        slot = kv[t][u].at[z * NX + frm]
        pltpu.make_async_copy(slot, slot, kx_recv.at[u, t, d - 1]).wait()

    def q_copy(u, d):
        to = lax.rem(x + d, NX)
        return pltpu.make_async_remote_copy(
            src_ref=q_src(u, to),
            dst_ref=qb[u].at[x],
            send_sem=q_send.at[u, d - 1],
            recv_sem=q_recv.at[u, d - 1],
            device_id=at_x(d),
            device_id_type=MESH,
        )

    carry = pltpu.make_async_remote_copy(
        src_ref=res_ref.at[0],
        dst_ref=car_ref,
        send_sem=car_send,
        recv_sem=car_recv,
        device_id=after,
        device_id_type=MESH,
    )
    for u in range(UNITS):
        for t in (0, 1):
            for d in (1, 2, 3):
                kx_copy(u, t, d).start()
    carry.start()
    for u in range(UNITS):
        for d in (1, 2, 3):
            q_copy(u, d).start()

    def rows(u, t, origin):
        return kv[t][u].at[pl.ds(lax.rem(origin + NZ, NZ) * NX, NX)]

    def z_copy(way, u, t, step):
        sign = 1 if way == 0 else -1
        part = rows(u, t, z - sign * step)
        return pltpu.make_async_remote_copy(
            src_ref=part,
            dst_ref=part,
            send_sem=z_send.at[way, u, t, step],
            recv_sem=z_recv.at[way, u, t, step],
            device_id=at_z(sign),
            device_id_type=MESH,
        )

    def z_arrived(way, u, t, step):
        sign = 1 if way == 0 else -1
        part = rows(u, t, z - sign * (step + 1))
        pltpu.make_async_copy(part, part, z_recv.at[way, u, t, step]).wait()

    row_ready = set()
    orders = [ring_order(0), ring_order(1)]
    places = len(orders[0][0])

    def place_step(p):
        for way in (0, 1):
            u, t, step = orders[way][0][p]
            if step == 0:
                if (u, t) not in row_ready:
                    row_ready.add((u, t))
                    own_copy(u, t).wait()
                    for d in (1, 2, 3):
                        kx_arrived(u, t, d)
            else:
                z_arrived(way, u, t, step - 1)
            z_copy(way, u, t, step).start()

    def last_place(u):
        return max(
            orders[way][1][u, t, HOPS[t, way] - 1] for way in (0, 1) for t in (0, 1)
        )

    def attend(u, b, first):
        i = z * NX + b
        q = qb[u].at[b]
        out = ob[u // 2].at[b]
        bias = []
        for m in range(NSEL):
            pick = pats[u, i, m]
            safe = jnp.maximum(pick, 0)
            ksel[pl.ds(m * BLOCK, BLOCK), :] = kv[0][u][safe]
            vsel[pl.ds(m * BLOCK, BLOCK), pl.ds(0, HD)] = kv[1][u][safe]
            bias.append(jnp.where(pick >= 0, 0.0, NEG).astype(jnp.float32))
        for h in range(GROUP):
            cols = pl.ds(h * HD, HD)
            scores = lax.dot_general(
                q[:, cols], ksel[...], (((1,), (1,)), ((), ())),
                preferred_element_type=jnp.float32,
            )
            parts = []
            for m in range(NSEL):
                part = scores[:, m * BLOCK : (m + 1) * BLOCK]
                parts.append(part + (diag[...] if m == 0 else bias[m]))
            top = parts[0]
            for part in parts[1:]:
                top = jnp.maximum(top, part)
            top = jnp.max(top, axis=1, keepdims=True)
            weights = jnp.concatenate(
                [jnp.exp2((part - top) * EXP2_SCALE).astype(jnp.bfloat16) for part in parts],
                axis=1,
            )
            mixed = jnp.dot(weights, vsel[...], preferred_element_type=jnp.float32)
            mixed = (mixed[:, :HD] / mixed[:, HD:]).astype(jnp.bfloat16)
            if first:
                out[:, cols] = mixed
            else:
                both = out[:, cols].astype(jnp.float32) + mixed.astype(jnp.float32)
                out[:, cols] = both.astype(jnp.bfloat16)

    def out_slot(cc, who):
        cols = pl.multiple_of((2 * who + cc) * WIDE, WIDE)
        return sum_ref.at[:, pl.ds(cols, WIDE)]

    def out_copy(cc, j, k):
        b = lax.rem(x + j, NX)
        return pltpu.make_async_remote_copy(
            src_ref=ob[cc].at[b],
            dst_ref=out_slot(cc, x),
            send_sem=o_send.at[cc, k],
            recv_sem=o_recv.at[cc, k],
            device_id=(seg, z * NX + b),
            device_id_type=MESH,
        )

    def out_own(cc):
        return pltpu.make_async_copy(ob[cc].at[x], out_slot(cc, x), o_own.at[cc])

    def unit(u, steps):
        cc, layer = u // 2, u % 2
        for t in (0, 1):
            for way in (0, 1):
                z_arrived(way, u, t, HOPS[t, way] - 1)
        pat_copy(u).wait()

        def one(k, _):
            for kk in range(NX):
                if steps[kk]:

                    @pl.when(k == kk)
                    def _():
                        for p in steps[kk]:
                            place_step(p)

            b = lax.rem(x + NX - 1 - k, NX)
            slot = qb[u].at[b]
            pltpu.make_async_copy(slot, slot, q_recv.at[u, k]).wait()
            attend(u, b, layer == 0)
            if layer == 1:

                @pl.when(k >= 1)
                def _():
                    out_copy(cc, NX - k, k - 1).start()

            return 0

        lax.fori_loop(0, NX, one, 0)
        if layer == 1:
            out_own(cc).start()

    done = 0
    for u in range(UNITS):
        start = min(last_place(u) + LAG, places)
        while done < start:
            place_step(done)
            done += 1
        limit = places if u + 1 == UNITS else min(last_place(u + 1) + LAG, places)
        steps = []
        for kk in range(NX):
            take = [done] if done < limit and kk else []
            done += len(take)
            steps.append(take)
        unit(u, steps)

    for cc in (0, 1):
        for k in range(NX - 1):
            slot = out_slot(cc, lax.rem(x + 1 + k, NX))
            pltpu.make_async_copy(slot, slot, o_recv.at[cc, k]).wait()
            out_copy(cc, NX - 1 - k, k).wait_send()
        out_own(cc).wait()
    carry.wait()
    for u in range(UNITS):
        for d in (1, 2, 3):
            q_copy(u, d).wait_send()
            for t in (0, 1):
                kx_copy(u, t, d).wait_send()
    for way in (0, 1):
        for u, t, step in orders[way][0]:
            z_copy(way, u, t, step).wait_send()


def local(residual, query_rows, key_rows, value_rows, pattern):
    tokens, width = residual.shape[1:]
    any_spec = pl.BlockSpec(memory_space=pl.ANY)
    dma = pltpu.SemaphoreType.DMA
    bf16 = jnp.bfloat16
    layer_sum, carried = pl.pallas_call(
        body,
        name="relay_attention",
        out_shape=[jax.ShapeDtypeStruct((tokens, width), bf16)] * 2,
        in_specs=[any_spec] * 5,
        out_specs=[any_spec] * 2,
        scratch_shapes=[pltpu.VMEM((NZ * NX, BLOCK, HD), bf16)] * 8
        + [pltpu.VMEM((NX, BLOCK, WIDE), bf16)] * 6
        + [
            pltpu.VMEM((NSEL * BLOCK, HD), bf16),
            pltpu.VMEM((NSEL * BLOCK, 2 * HD), bf16),
            pltpu.VMEM((BLOCK, BLOCK), jnp.float32),
            pltpu.SMEM((UNITS, NZ * NX, NSEL), jnp.int32),
            dma((UNITS, 2, 3)), dma((UNITS, 2, 3)), dma((UNITS, 2)),
            dma((2, UNITS, 2, 4)), dma((2, UNITS, 2, 4)),
            dma((UNITS, 3)), dma((UNITS, 4)),
            dma((2, 3)), dma((2, 3)), dma((2,)),
            dma((UNITS,)), dma(()), dma(()),
        ],
        compiler_params=pltpu.CompilerParams(
            collective_id=0, has_side_effects=True, vmem_limit_bytes=60 * 2**20
        ),
    )(pattern, residual, query_rows, key_rows, value_rows)
    out = carried.astype(jnp.float32) + layer_sum.astype(jnp.float32)
    return out[None]


def solution(mesh):
    return jax.shard_map(
        local,
        mesh=mesh,
        in_specs=(
            P("segment", "seq", None),
            P("segment", None, "seq", None),
            P("segment", None, "seq", None),
            P("segment", None, "seq", None),
            P("segment", None, None, None, None),
        ),
        out_specs=P("segment", "seq", None),
        check_vma=False,
    )
```

```python
import math

import jax
import jax.numpy as jnp
from jax import lax
from jax.experimental import pallas as pl
from jax.experimental.pallas import tpu as pltpu
from jax.sharding import PartitionSpec as P

HQ = 64
HK = 8
HD = 128
LAYERS = 2
BLOCK = 128
NSEL = 8
NZ = 8
NX = 4
UNITS = 4
GROUP = HQ // HK
WIDE = GROUP * HD
EXP2_SCALE = math.log2(math.e) / math.sqrt(HD)
NEG = -1e30
MESH = pl.DeviceIdType.MESH
TOGETHER = 4

CHUNKS = (0, 4, 1, 5, 2, 3, 6, 7)
EARLY = CHUNKS[:4]
ORDERS = (
    (0, 4, 1, 0, 5, 0, 6, 0, 1, 4, 2, 4, 2, 1, 5, 1, 5, 3, 2, 3, 2, 3, 6, 7, 6, 7, 6, 7),
    (0, 4, 1, 4, 5, 4, 2, 0, 3, 1, 0, 4, 5, 3, 5, 1, 5, 2, 3, 2, 3, 7, 6, 7, 6, 7, 6, 7),
)
KEYS, VALUES, BOTH = (0,), (1,), (0, 1)
WORK = (
    (14, BOTH, 0, {4: 1, 7: 1}),
    (19, BOTH, 1, {4: 1, 7: 1}),
    (23, KEYS, 2, {5: 1}),
    (0, KEYS, 3, {1: 1, 5: 1}),
    (28, VALUES, 2, {}),
    (28, VALUES, 3, {}),
)


def split(chunk):
    return chunk % UNITS, chunk // UNITS


def ring_order(way):
    seen = [0] * 2 * UNITS
    order = []
    for chunk in ORDERS[way]:
        order.append((*split(chunk), seen[chunk]))
        seen[chunk] += 1
    return order, seen


def body(
    pat_ref, res_ref, q_ref, k_ref, v_ref, sum_ref, car_ref,
    kb0, kb1, kb2, kb3, vb0, vb1, vb2, vb3, qb0, qb1, qb2, qb3, ob0, ob1,
    pb2, pb3, ksel, vsel, diag, pats,
    kx_send, kx_recv, own_sem, z_send, z_recv, e_send, e_recv, q_send, q_recv, o_send, o_recv, o_own,
    pat_sem, car_send, car_recv,
):
    kv = ((kb0, kb1, kb2, kb3), (vb0, vb1, vb2, vb3))
    kv_in = (k_ref, v_ref)
    qb = (qb0, qb1, qb2, qb3)
    ob = (ob0, ob1)
    pb = {2: pb2, 3: pb3}
    seg = lax.axis_index("segment")
    me = lax.axis_index("seq")
    z = me // NX
    x = lax.rem(me, NX)
    nseg = lax.axis_size("segment")

    def at_x(d):
        return (seg, z * NX + lax.rem(x + d, NX))

    def at_z(d):
        return (seg, lax.rem(z + d + NZ, NZ) * NX + x)

    after = (lax.rem(seg + 1, nseg), me)
    before = (lax.rem(seg + nseg - 1, nseg), me)

    def pat_copy(u):
        return pltpu.make_async_copy(
            pat_ref.at[0, u % 2, 2 * x + u // 2], pats.at[u], pat_sem.at[u]
        )

    def kv_src(u, t, who):
        cols = pl.multiple_of((2 * who + u // 2) * HD, HD)
        return kv_in[t].at[0, u % 2, :, pl.ds(cols, HD)]

    def q_src(u, who):
        cols = pl.multiple_of((2 * who + u // 2) * WIDE, WIDE)
        return q_ref.at[0, u % 2, :, pl.ds(cols, WIDE)]

    def own_copy(u, t):
        return pltpu.make_async_copy(
            kv_src(u, t, x), kv[t][u].at[z * NX + x], own_sem.at[u, t]
        )

    def own_q(u):
        return pltpu.make_async_copy(q_src(u, x), qb[u].at[x], q_recv.at[u, NX - 1])

    barrier = pltpu.get_barrier_semaphore()
    peers = [at_x(1), at_x(2), at_x(3), at_z(1), at_z(-1), after, before]
    for peer in peers:
        pl.semaphore_signal(barrier, inc=1, device_id=peer, device_id_type=MESH)
    for u in range(UNITS):
        for t in (0, 1):
            own_copy(u, t).start()
    for u in range(UNITS):
        pat_copy(u).start()
        own_q(u).start()
    row = lax.broadcasted_iota(jnp.int32, (BLOCK, BLOCK), 0)
    col = lax.broadcasted_iota(jnp.int32, (BLOCK, BLOCK), 1)
    diag[...] = jnp.where(row >= col, 0.0, NEG).astype(jnp.float32)
    vsel[:, pl.ds(HD, HD)] = jnp.ones((NSEL * BLOCK, HD), jnp.bfloat16)
    pl.semaphore_wait(barrier, len(peers))

    def kx_copy(u, t, d):
        to = lax.rem(x + d, NX)
        return pltpu.make_async_remote_copy(
            src_ref=kv_src(u, t, to),
            dst_ref=kv[t][u].at[z * NX + x],
            send_sem=kx_send.at[u, t, d - 1],
            recv_sem=kx_recv.at[u, t, d - 1],
            device_id=at_x(d),
            device_id_type=MESH,
        )

    def kx_arrived(u, t, d):
        frm = lax.rem(x + NX - d, NX)
        slot = kv[t][u].at[z * NX + frm]
        pltpu.make_async_copy(slot, slot, kx_recv.at[u, t, d - 1]).wait()

    def q_copy(u, d):
        to = lax.rem(x + d, NX)
        return pltpu.make_async_remote_copy(
            src_ref=q_src(u, to),
            dst_ref=qb[u].at[x],
            send_sem=q_send.at[u, d - 1],
            recv_sem=q_recv.at[u, d - 1],
            device_id=at_x(d),
            device_id_type=MESH,
        )

    carry = pltpu.make_async_remote_copy(
        src_ref=res_ref.at[0],
        dst_ref=car_ref,
        send_sem=car_send,
        recv_sem=car_recv,
        device_id=after,
        device_id_type=MESH,
    )
    chunks = [split(chunk) for chunk in CHUNKS]
    early = [split(chunk) for chunk in EARLY]

    def early_copy(way, u, t, d):
        part = kv[t][u].at[z * NX + lax.rem(x + NX - d, NX)]
        return pltpu.make_async_remote_copy(
            src_ref=part,
            dst_ref=part,
            send_sem=e_send.at[way, u, t, d],
            recv_sem=e_recv.at[way, u, t, d],
            device_id=at_z(1 if way == 0 else -1),
            device_id_type=MESH,
        )

    def early_arrived(way, u, t, d):
        origin = lax.rem(z + (NZ - 1 if way == 0 else 1), NZ)
        part = kv[t][u].at[origin * NX + lax.rem(x + NX - d, NX)]
        pltpu.make_async_copy(part, part, e_recv.at[way, u, t, d]).wait()

    for n, (u, t) in enumerate(chunks):
        for d in (1, 2, 3):
            kx_copy(u, t, d).start()
        if (u, t) in early:
            own_copy(u, t).wait()
            for way in (0, 1):
                early_copy(way, u, t, 0).start()
    carry.start()
    for u in range(UNITS):
        for d in (1, 2, 3):
            q_copy(u, d).start()

    def rows(u, t, origin):
        return kv[t][u].at[pl.ds(lax.rem(origin + NZ, NZ) * NX, NX)]

    def z_copy(way, u, t, step):
        sign = 1 if way == 0 else -1
        part = rows(u, t, z - sign * step)
        return pltpu.make_async_remote_copy(
            src_ref=part,
            dst_ref=part,
            send_sem=z_send.at[way, u, t, step],
            recv_sem=z_recv.at[way, u, t, step],
            device_id=at_z(sign),
            device_id_type=MESH,
        )

    def z_arrived(way, u, t, step):
        if step == 0 and (u, t) in early:
            for d in range(NX):
                early_arrived(way, u, t, d)
            return
        sign = 1 if way == 0 else -1
        part = rows(u, t, z - sign * (step + 1))
        pltpu.make_async_copy(part, part, z_recv.at[way, u, t, step]).wait()

    orders = [ring_order(0), ring_order(1)]
    places = len(orders[0][0])
    opens = {}
    for p in range(places):
        for way in (0, 1):
            u, t, step = orders[way][0][p]
            opens.setdefault((u, t), (p, way))

    def place_step(p):
        for way in (0, 1):
            u, t, step = orders[way][0][p]
            if step == 0:
                if opens[u, t] == (p, way):
                    if (u, t) not in early:
                        own_copy(u, t).wait()
                    for d in (1, 2, 3):
                        kx_arrived(u, t, d)
            else:
                z_arrived(way, u, t, step - 1)
            if step == 0 and (u, t) in early:
                for d in (1, 2, 3):
                    early_copy(way, u, t, d).start()
            else:
                z_copy(way, u, t, step).start()

    def whole(u, t):
        for way in (0, 1):
            z_arrived(way, u, t, orders[way][1][t * UNITS + u] - 1)

    def picks(u, b):
        return [pats[u, m, z * NX + b] for m in range(NSEL)]

    def take_keys(u, chosen):
        bias = []
        for m, pick in enumerate(chosen):
            ksel[pl.ds(m * BLOCK, BLOCK), :] = kv[0][u][jnp.maximum(pick, 0)]
            bias.append(jnp.where(pick >= 0, 0.0, NEG).astype(jnp.float32))
        return bias

    def take_values(u, chosen):
        for m, pick in enumerate(chosen):
            vsel[pl.ds(m * BLOCK, BLOCK), pl.ds(0, HD)] = kv[1][u][jnp.maximum(pick, 0)]

    def weigh(u, b, h, bias):
        scores = lax.dot_general(
            qb[u].at[b][:, pl.ds(h * HD, HD)], ksel[...], (((1,), (1,)), ((), ())),
            preferred_element_type=jnp.float32,
        )
        parts = []
        for m in range(NSEL):
            part = scores[:, m * BLOCK : (m + 1) * BLOCK]
            parts.append(part + (diag[...] if m == 0 else bias[m]))
        top = parts[0]
        for part in parts[1:]:
            top = jnp.maximum(top, part)
        top = jnp.max(top, axis=1, keepdims=True)
        return jnp.concatenate(
            [jnp.exp2((part - top) * EXP2_SCALE).astype(jnp.bfloat16) for part in parts],
            axis=1,
        )

    def mix(u, b, h, weights):
        out = ob[u // 2].at[b]
        mixed = jnp.dot(weights, vsel[...], preferred_element_type=jnp.float32)
        mixed = (mixed[:, :HD] / mixed[:, HD:]).astype(jnp.bfloat16)
        for n in range(weights.shape[0] // BLOCK):
            cols = pl.ds((h + n) * HD, HD)
            one = mixed[n * BLOCK : (n + 1) * BLOCK]
            if u % 2:
                one = (out[:, cols].astype(jnp.float32) + one.astype(jnp.float32)).astype(
                    jnp.bfloat16
                )
            out[:, cols] = one

    def out_slot(cc, who):
        cols = pl.multiple_of((2 * who + cc) * WIDE, WIDE)
        return sum_ref.at[:, pl.ds(cols, WIDE)]

    def out_copy(cc, j, k):
        b = lax.rem(x + j, NX)
        return pltpu.make_async_remote_copy(
            src_ref=ob[cc].at[b],
            dst_ref=out_slot(cc, x),
            send_sem=o_send.at[cc, k],
            recv_sem=o_recv.at[cc, k],
            device_id=(seg, z * NX + b),
            device_id_type=MESH,
        )

    def out_own(cc):
        return pltpu.make_async_copy(ob[cc].at[x], out_slot(cc, x), o_own.at[cc])

    def blocks(run, steps):
        def one(k, _):
            b = lax.rem(x + NX - 1 - k, NX)
            kept = None
            for half in (0, 1):
                for kk in range(NX):
                    due = steps.get((kk, half), ())
                    if due:

                        @pl.when(k == kk)
                        def _():
                            for p in due:
                                place_step(p)

                kept = run(k, b, half, kept)
            return 0

        lax.fori_loop(0, NX, one, 0)

    def arrived_q(u, b, k):
        slot = qb[u].at[b]
        pltpu.make_async_copy(slot, slot, q_recv.at[u, k]).wait()

    half_heads = GROUP // 2

    def send_before(cc, k):
        @pl.when(k >= 1)
        def _():
            out_copy(cc, NX - k, k - 1).start()

    def run_both(u):
        def run(k, b, half, kept):
            if half == 0:
                arrived_q(u, b, k)
                chosen = picks(u, b)
                kept = take_keys(u, chosen)
                take_values(u, chosen)
            for h in range(half * half_heads, (half + 1) * half_heads):
                mix(u, b, h, weigh(u, b, h, kept))
            if half == 1 and u % 2 == 1:
                send_before(u // 2, k)
            return kept

        return run

    def run_weights(u):
        def run(k, b, half, kept):
            if half == 0:
                arrived_q(u, b, k)
                kept = take_keys(u, picks(u, b))
            for h in range(half * half_heads, (half + 1) * half_heads):
                pb[u][b, pl.ds(h * BLOCK, BLOCK), :] = weigh(u, b, h, kept)
            return kept

        return run

    def run_values(u):
        def run(k, b, half, kept):
            if half == 0:
                take_values(u, picks(u, b))
            for h in range(half * half_heads, (half + 1) * half_heads, TOGETHER):
                mix(u, b, h, pb[u][b, pl.ds(h * BLOCK, TOGETHER * BLOCK), :])
            if half == 1 and u % 2 == 1:
                send_before(u // 2, k)
            return kept

        return run

    done = 0

    def catch_up(to):
        nonlocal done
        while done < min(to, places):
            place_step(done)
            done += 1

    for u in range(UNITS):
        pat_copy(u).wait()
    runs = {KEYS: run_weights, VALUES: run_values, BOTH: run_both}
    for before, kinds, u, pauses in WORK:
        catch_up(before)
        for kind in kinds:
            whole(u, kind)
        steps = {}
        for at, count in pauses.items():
            steps[divmod(at, 2)] = range(done, done + count)
            done += count
        blocks(runs[kinds](u), steps)
        if u % 2 and kinds != KEYS:
            out_own(u // 2).start()

    for cc in (0, 1):
        for k in range(NX - 1):
            slot = out_slot(cc, lax.rem(x + 1 + k, NX))
            pltpu.make_async_copy(slot, slot, o_recv.at[cc, k]).wait()
            out_copy(cc, NX - 1 - k, k).wait_send()
        out_own(cc).wait()
    carry.wait()
    for u in range(UNITS):
        for d in (1, 2, 3):
            q_copy(u, d).wait_send()
            for t in (0, 1):
                kx_copy(u, t, d).wait_send()
    for way in (0, 1):
        for u, t, step in orders[way][0]:
            if step == 0 and (u, t) in early:
                for d in range(NX):
                    early_copy(way, u, t, d).wait_send()
            else:
                z_copy(way, u, t, step).wait_send()


def local(residual, query_rows, key_rows, value_rows, pattern):
    tokens, width = residual.shape[1:]
    any_spec = pl.BlockSpec(memory_space=pl.ANY)
    dma = pltpu.SemaphoreType.DMA
    bf16 = jnp.bfloat16
    layer_sum, carried = pl.pallas_call(
        body,
        name="relay_attention",
        out_shape=[pltpu.VMEM((tokens, width), bf16)] * 2,
        in_specs=[any_spec] * 5,
        out_specs=[pl.BlockSpec(memory_space=pltpu.VMEM)] * 2,
        scratch_shapes=[pltpu.VMEM((NZ * NX, BLOCK, HD), bf16)] * 8
        + [pltpu.VMEM((NX, BLOCK, WIDE), bf16)] * 6
        + [pltpu.VMEM((NX, GROUP * BLOCK, NSEL * BLOCK), bf16)] * 2
        + [
            pltpu.VMEM((NSEL * BLOCK, HD), bf16),
            pltpu.VMEM((NSEL * BLOCK, 2 * HD), bf16),
            pltpu.VMEM((BLOCK, BLOCK), jnp.float32),
            pltpu.SMEM((UNITS, NSEL, NZ * NX), jnp.int32),
            dma((UNITS, 2, 3)), dma((UNITS, 2, 3)), dma((UNITS, 2)),
            dma((2, UNITS, 2, 4)), dma((2, UNITS, 2, 4)),
            dma((2, UNITS, 2, NX)), dma((2, UNITS, 2, NX)),
            dma((UNITS, 3)), dma((UNITS, 4)),
            dma((2, 3)), dma((2, 3)), dma((2,)),
            dma((UNITS,)), dma(()), dma(()),
        ],
        compiler_params=pltpu.CompilerParams(
            collective_id=0, has_side_effects=True, vmem_limit_bytes=58 * 2**20
        ),
    )(jnp.swapaxes(pattern, 3, 4), residual, query_rows, key_rows, value_rows)
    out = carried.astype(jnp.float32) + layer_sum.astype(jnp.float32)
    return out[None]


def solution(mesh):
    return jax.shard_map(
        local,
        mesh=mesh,
        in_specs=(
            P("segment", "seq", None),
            P("segment", None, "seq", None),
            P("segment", None, "seq", None),
            P("segment", None, "seq", None),
            P("segment", None, None, None, None),
        ),
        out_specs=P("segment", "seq", None),
        check_vma=False,
    )
```

```python
import math

import jax
import jax.numpy as jnp
from jax import lax
from jax.experimental import pallas as pl
from jax.experimental.pallas import tpu as pltpu
from jax.sharding import PartitionSpec as P

HQ = 64
HK = 8
HD = 128
LAYERS = 2
BLOCK = 128
NSEL = 8
NZ = 8
NX = 4
UNITS = 4
GROUP = HQ // HK
WIDE = GROUP * HD
EXP2_SCALE = math.log2(math.e) / math.sqrt(HD)
NEG = -1e30
MESH = pl.DeviceIdType.MESH
TOGETHER = 4

CHUNKS = (0, 4, 1, 5, 2, 3, 6, 7)
EARLY = CHUNKS[:4]
ORDERS = (
    (0, 4, 1, 0, 5, 0, 6, 0, 1, 4, 2, 4, 2, 1, 5, 1, 5, 3, 2, 3, 2, 3, 6, 7, 6, 7, 6, 7),
    (0, 4, 1, 4, 5, 4, 2, 0, 3, 1, 0, 4, 5, 3, 5, 1, 5, 2, 3, 2, 3, 7, 6, 7, 6, 7, 6, 7),
)
KEYS, VALUES, BOTH = (0,), (1,), (0, 1)
WORK = (
    (14, BOTH, 0, {4: 1, 7: 1}),
    (19, BOTH, 1, {4: 1, 7: 1}),
    (23, KEYS, 2, {5: 1}),
    (0, KEYS, 3, {1: 1, 5: 1}),
    (28, VALUES, 2, {}),
    (28, VALUES, 3, {}),
)


def split(chunk):
    return chunk % UNITS, chunk // UNITS


def ring_order(way):
    seen = [0] * 2 * UNITS
    order = []
    for chunk in ORDERS[way]:
        order.append((*split(chunk), seen[chunk]))
        seen[chunk] += 1
    return order, seen


def body(
    pat_ref, res_ref, q_ref, k_ref, v_ref, sum_ref, car_ref,
    kb0, kb1, kb2, kb3, vb0, vb1, vb2, vb3, qb0, qb1, qb2, qb3, ob0, ob1,
    pb2, pb3, ksel, vsel, diag, pats,
    kx_send, kx_recv, own_sem, z_send, z_recv, e_send, e_recv, q_send, q_recv, o_send, o_recv, o_own,
    pat_sem, car_send, car_recv,
):
    kv = ((kb0, kb1, kb2, kb3), (vb0, vb1, vb2, vb3))
    kv_in = (k_ref, v_ref)
    qb = (qb0, qb1, qb2, qb3)
    ob = (ob0, ob1)
    pb = {2: pb2, 3: pb3}
    seg = lax.axis_index("segment")
    me = lax.axis_index("seq")
    z = me // NX
    x = lax.rem(me, NX)
    nseg = lax.axis_size("segment")

    def at_x(d):
        return (seg, z * NX + lax.rem(x + d, NX))

    def at_z(d):
        return (seg, lax.rem(z + d + NZ, NZ) * NX + x)

    after = (lax.rem(seg + 1, nseg), me)
    before = (lax.rem(seg + nseg - 1, nseg), me)

    def pat_copy(u):
        return pltpu.make_async_copy(
            pat_ref.at[0, u % 2, 2 * x + u // 2], pats.at[u], pat_sem.at[u]
        )

    def kv_src(u, t, who):
        cols = pl.multiple_of((2 * who + u // 2) * HD, HD)
        return kv_in[t].at[0, u % 2, :, pl.ds(cols, HD)]

    def q_src(u, who):
        cols = pl.multiple_of((2 * who + u // 2) * WIDE, WIDE)
        return q_ref.at[0, u % 2, :, pl.ds(cols, WIDE)]

    def own_copy(u, t):
        return pltpu.make_async_copy(
            kv_src(u, t, x), kv[t][u].at[z * NX + x], own_sem.at[u, t]
        )

    def own_q(u):
        return pltpu.make_async_copy(q_src(u, x), qb[u].at[x], q_recv.at[u, NX - 1])

    barrier = pltpu.get_barrier_semaphore()
    peers = [at_x(1), at_x(2), at_x(3), at_z(1), at_z(-1), after, before]
    for peer in peers:
        pl.semaphore_signal(barrier, inc=1, device_id=peer, device_id_type=MESH)
    for u in range(UNITS):
        for t in (0, 1):
            own_copy(u, t).start()
    for u in range(UNITS):
        pat_copy(u).start()
        own_q(u).start()
    row = lax.broadcasted_iota(jnp.int32, (BLOCK, BLOCK), 0)
    col = lax.broadcasted_iota(jnp.int32, (BLOCK, BLOCK), 1)
    diag[...] = jnp.where(row >= col, 0.0, NEG).astype(jnp.float32)
    vsel[:, pl.ds(HD, HD)] = jnp.ones((NSEL * BLOCK, HD), jnp.bfloat16)
    pl.semaphore_wait(barrier, len(peers))

    def kx_copy(u, t, d):
        to = lax.rem(x + d, NX)
        return pltpu.make_async_remote_copy(
            src_ref=kv_src(u, t, to),
            dst_ref=kv[t][u].at[z * NX + x],
            send_sem=kx_send.at[u, t, d - 1],
            recv_sem=kx_recv.at[u, t, d - 1],
            device_id=at_x(d),
            device_id_type=MESH,
        )

    def kx_arrived(u, t, d):
        frm = lax.rem(x + NX - d, NX)
        slot = kv[t][u].at[z * NX + frm]
        pltpu.make_async_copy(slot, slot, kx_recv.at[u, t, d - 1]).wait()

    def q_copy(u, d):
        to = lax.rem(x + d, NX)
        return pltpu.make_async_remote_copy(
            src_ref=q_src(u, to),
            dst_ref=qb[u].at[x],
            send_sem=q_send.at[u, d - 1],
            recv_sem=q_recv.at[u, d - 1],
            device_id=at_x(d),
            device_id_type=MESH,
        )

    carry = pltpu.make_async_remote_copy(
        src_ref=res_ref.at[0],
        dst_ref=car_ref,
        send_sem=car_send,
        recv_sem=car_recv,
        device_id=after,
        device_id_type=MESH,
    )
    chunks = [split(chunk) for chunk in CHUNKS]
    early = [split(chunk) for chunk in EARLY]

    def early_copy(way, u, t, d):
        part = kv[t][u].at[z * NX + lax.rem(x + NX - d, NX)]
        return pltpu.make_async_remote_copy(
            src_ref=part,
            dst_ref=part,
            send_sem=e_send.at[way, u, t, d],
            recv_sem=e_recv.at[way, u, t, d],
            device_id=at_z(1 if way == 0 else -1),
            device_id_type=MESH,
        )

    def early_arrived(way, u, t, d):
        origin = lax.rem(z + (NZ - 1 if way == 0 else 1), NZ)
        part = kv[t][u].at[origin * NX + lax.rem(x + NX - d, NX)]
        pltpu.make_async_copy(part, part, e_recv.at[way, u, t, d]).wait()


    def rows(u, t, origin):
        return kv[t][u].at[pl.ds(lax.rem(origin + NZ, NZ) * NX, NX)]

    def z_copy(way, u, t, step):
        sign = 1 if way == 0 else -1
        part = rows(u, t, z - sign * step)
        return pltpu.make_async_remote_copy(
            src_ref=part,
            dst_ref=part,
            send_sem=z_send.at[way, u, t, step],
            recv_sem=z_recv.at[way, u, t, step],
            device_id=at_z(sign),
            device_id_type=MESH,
        )

    def z_arrived(way, u, t, step):
        if step == 0 and (u, t) in early:
            for d in range(NX):
                early_arrived(way, u, t, d)
            return
        sign = 1 if way == 0 else -1
        part = rows(u, t, z - sign * (step + 1))
        pltpu.make_async_copy(part, part, z_recv.at[way, u, t, step]).wait()

    orders = [ring_order(0), ring_order(1)]
    places = len(orders[0][0])

    def hops(way, u, t):
        return orders[way][1][t * UNITS + u]

    def sends(way, u, t, step):
        if way == 0:
            return jnp.logical_and(z >= step, z < NZ - 1)
        return lax.rem(z + step, NZ) < hops(way, u, t)

    def receives(way, u, t, step):
        if way == 0:
            return z > step
        return lax.rem(z + 1 + step, NZ) < hops(way, u, t)

    opens = {}
    for p in range(places):
        for way in (0, 1):
            u, t, step = orders[way][0][p]
            opens.setdefault((u, t), (p, way))

    for u, t in chunks:
        for d in (1, 2, 3):
            kx_copy(u, t, d).start()
        if (u, t) in early:
            own_copy(u, t).wait()
            for way in (0, 1):

                @pl.when(sends(way, u, t, 0))
                def _():
                    early_copy(way, u, t, 0).start()

    carry.start()
    for u in range(UNITS):
        for d in (1, 2, 3):
            q_copy(u, d).start()

    def place_step(p):
        for way in (0, 1):
            u, t, step = orders[way][0][p]
            if step == 0:
                if opens[u, t] == (p, way):
                    if (u, t) not in early:
                        own_copy(u, t).wait()
                    for d in (1, 2, 3):
                        kx_arrived(u, t, d)

            @pl.when(sends(way, u, t, step))
            def _():
                if step:
                    z_arrived(way, u, t, step - 1)
                if step == 0 and (u, t) in early:
                    for d in (1, 2, 3):
                        early_copy(way, u, t, d).start()
                else:
                    z_copy(way, u, t, step).start()

    def whole(u, t):
        for way in (0, 1):
            for step in range(hops(way, u, t)):
                ends = receives(way, u, t, step)
                if step + 1 < hops(way, u, t):
                    ends = jnp.logical_and(ends, jnp.logical_not(sends(way, u, t, step + 1)))

                @pl.when(ends)
                def _():
                    z_arrived(way, u, t, step)

    def picks(u, b):
        return [pats[u, m, z * NX + b] for m in range(NSEL)]

    def take_keys(u, chosen):
        bias = []
        for m, pick in enumerate(chosen):
            ksel[pl.ds(m * BLOCK, BLOCK), :] = kv[0][u][jnp.maximum(pick, 0)]
            bias.append(jnp.where(pick >= 0, 0.0, NEG).astype(jnp.float32))
        return bias

    def take_values(u, chosen):
        for m, pick in enumerate(chosen):
            vsel[pl.ds(m * BLOCK, BLOCK), pl.ds(0, HD)] = kv[1][u][jnp.maximum(pick, 0)]

    def weigh(u, b, h, bias):
        scores = lax.dot_general(
            qb[u].at[b][:, pl.ds(h * HD, HD)], ksel[...], (((1,), (1,)), ((), ())),
            preferred_element_type=jnp.float32,
        )
        parts = []
        for m in range(NSEL):
            part = scores[:, m * BLOCK : (m + 1) * BLOCK]
            parts.append(part + (diag[...] if m == 0 else bias[m]))
        top = parts[0]
        for part in parts[1:]:
            top = jnp.maximum(top, part)
        top = jnp.max(top, axis=1, keepdims=True)
        return jnp.concatenate(
            [jnp.exp2((part - top) * EXP2_SCALE).astype(jnp.bfloat16) for part in parts],
            axis=1,
        )

    def mix(u, b, h, weights):
        out = ob[u // 2].at[b]
        mixed = jnp.dot(weights, vsel[...], preferred_element_type=jnp.float32)
        mixed = (mixed[:, :HD] / mixed[:, HD:]).astype(jnp.bfloat16)
        for n in range(weights.shape[0] // BLOCK):
            cols = pl.ds((h + n) * HD, HD)
            one = mixed[n * BLOCK : (n + 1) * BLOCK]
            if u % 2:
                one = (out[:, cols].astype(jnp.float32) + one.astype(jnp.float32)).astype(
                    jnp.bfloat16
                )
            out[:, cols] = one

    def out_slot(cc, who):
        cols = pl.multiple_of((2 * who + cc) * WIDE, WIDE)
        return sum_ref.at[:, pl.ds(cols, WIDE)]

    def out_copy(cc, j, k):
        b = lax.rem(x + j, NX)
        return pltpu.make_async_remote_copy(
            src_ref=ob[cc].at[b],
            dst_ref=out_slot(cc, x),
            send_sem=o_send.at[cc, k],
            recv_sem=o_recv.at[cc, k],
            device_id=(seg, z * NX + b),
            device_id_type=MESH,
        )

    def out_own(cc):
        return pltpu.make_async_copy(ob[cc].at[x], out_slot(cc, x), o_own.at[cc])

    def blocks(run, steps):
        def one(k, _):
            b = lax.rem(x + NX - 1 - k, NX)
            kept = None
            for half in (0, 1):
                for kk in range(NX):
                    due = steps.get((kk, half), ())
                    if due:

                        @pl.when(k == kk)
                        def _():
                            for p in due:
                                place_step(p)

                kept = run(k, b, half, kept)
            return 0

        lax.fori_loop(0, NX, one, 0)

    def arrived_q(u, b, k):
        slot = qb[u].at[b]
        pltpu.make_async_copy(slot, slot, q_recv.at[u, k]).wait()

    half_heads = GROUP // 2

    def send_before(cc, k):
        @pl.when(k >= 1)
        def _():
            out_copy(cc, NX - k, k - 1).start()

    def run_both(u):
        def run(k, b, half, kept):
            if half == 0:
                arrived_q(u, b, k)
                chosen = picks(u, b)
                kept = take_keys(u, chosen)
                take_values(u, chosen)
            for h in range(half * half_heads, (half + 1) * half_heads):
                mix(u, b, h, weigh(u, b, h, kept))
            if half == 1 and u % 2 == 1:
                send_before(u // 2, k)
            return kept

        return run

    def run_weights(u):
        def run(k, b, half, kept):
            if half == 0:
                arrived_q(u, b, k)
                kept = take_keys(u, picks(u, b))
            for h in range(half * half_heads, (half + 1) * half_heads):
                pb[u][b, pl.ds(h * BLOCK, BLOCK), :] = weigh(u, b, h, kept)
            return kept

        return run

    def run_values(u):
        def run(k, b, half, kept):
            if half == 0:
                take_values(u, picks(u, b))
            for h in range(half * half_heads, (half + 1) * half_heads, TOGETHER):
                mix(u, b, h, pb[u][b, pl.ds(h * BLOCK, TOGETHER * BLOCK), :])
            if half == 1 and u % 2 == 1:
                send_before(u // 2, k)
            return kept

        return run

    done = 0

    def catch_up(to):
        nonlocal done
        while done < min(to, places):
            place_step(done)
            done += 1

    for u in range(UNITS):
        pat_copy(u).wait()
    runs = {KEYS: run_weights, VALUES: run_values, BOTH: run_both}
    for before, kinds, u, pauses in WORK:
        catch_up(before)
        for kind in kinds:
            whole(u, kind)
        steps = {}
        for at, count in pauses.items():
            steps[divmod(at, 2)] = range(done, done + count)
            done += count
        blocks(runs[kinds](u), steps)
        if u % 2 and kinds != KEYS:
            out_own(u // 2).start()

    for cc in (0, 1):
        for k in range(NX - 1):
            slot = out_slot(cc, lax.rem(x + 1 + k, NX))
            pltpu.make_async_copy(slot, slot, o_recv.at[cc, k]).wait()
            out_copy(cc, NX - 1 - k, k).wait_send()
        out_own(cc).wait()
    carry.wait()
    for u in range(UNITS):
        for d in (1, 2, 3):
            q_copy(u, d).wait_send()
            for t in (0, 1):
                kx_copy(u, t, d).wait_send()
    for way in (0, 1):
        for u, t, step in orders[way][0]:

            @pl.when(sends(way, u, t, step))
            def _():
                if step == 0 and (u, t) in early:
                    for d in range(NX):
                        early_copy(way, u, t, d).wait_send()
                else:
                    z_copy(way, u, t, step).wait_send()


def local(residual, query_rows, key_rows, value_rows, pattern):
    tokens, width = residual.shape[1:]
    any_spec = pl.BlockSpec(memory_space=pl.ANY)
    dma = pltpu.SemaphoreType.DMA
    bf16 = jnp.bfloat16
    layer_sum, carried = pl.pallas_call(
        body,
        name="relay_attention",
        out_shape=[pltpu.VMEM((tokens, width), bf16)] * 2,
        in_specs=[any_spec] * 5,
        out_specs=[pl.BlockSpec(memory_space=pltpu.VMEM)] * 2,
        scratch_shapes=[pltpu.VMEM((NZ * NX, BLOCK, HD), bf16)] * 8
        + [pltpu.VMEM((NX, BLOCK, WIDE), bf16)] * 6
        + [pltpu.VMEM((NX, GROUP * BLOCK, NSEL * BLOCK), bf16)] * 2
        + [
            pltpu.VMEM((NSEL * BLOCK, HD), bf16),
            pltpu.VMEM((NSEL * BLOCK, 2 * HD), bf16),
            pltpu.VMEM((BLOCK, BLOCK), jnp.float32),
            pltpu.SMEM((UNITS, NSEL, NZ * NX), jnp.int32),
            dma((UNITS, 2, 3)), dma((UNITS, 2, 3)), dma((UNITS, 2)),
            dma((2, UNITS, 2, 4)), dma((2, UNITS, 2, 4)),
            dma((2, UNITS, 2, NX)), dma((2, UNITS, 2, NX)),
            dma((UNITS, 3)), dma((UNITS, 4)),
            dma((2, 3)), dma((2, 3)), dma((2,)),
            dma((UNITS,)), dma(()), dma(()),
        ],
        compiler_params=pltpu.CompilerParams(
            collective_id=0, has_side_effects=True, vmem_limit_bytes=58 * 2**20
        ),
    )(jnp.swapaxes(pattern, 3, 4), residual, query_rows, key_rows, value_rows)
    out = carried.astype(jnp.float32) + layer_sum.astype(jnp.float32)
    return out[None]


def solution(mesh):
    return jax.shard_map(
        local,
        mesh=mesh,
        in_specs=(
            P("segment", "seq", None),
            P("segment", None, "seq", None),
            P("segment", None, "seq", None),
            P("segment", None, "seq", None),
            P("segment", None, None, None, None),
        ),
        out_specs=P("segment", "seq", None),
        check_vma=False,
    )
```

```python
import math

import jax
import jax.numpy as jnp
from jax import lax
from jax.experimental import pallas as pl
from jax.experimental.pallas import tpu as pltpu
from jax.sharding import PartitionSpec as P

HQ = 64
HK = 8
HD = 128
LAYERS = 2
BLOCK = 128
NSEL = 8
NZ = 8
NX = 4
UNITS = 4
GROUP = HQ // HK
WIDE = GROUP * HD
EXP2_SCALE = math.log2(math.e) / math.sqrt(HD)
NEG = -1e30
MESH = pl.DeviceIdType.MESH
TOGETHER = 4

CHUNKS = (0, 4, 1, 5, 2, 3, 6, 7)
EARLY = CHUNKS[:4]
ORDERS = (
    (0, 4, 1, 0, 5, 0, 6, 0, 1, 4, 2, 4, 2, 1, 5, 1, 5, 3, 2, 3, 2, 3, 6, 7, 6, 7, 6, 7),
    (0, 4, 1, 4, 5, 4, 2, 0, 3, 1, 0, 4, 5, 3, 5, 1, 5, 2, 3, 2, 3, 7, 6, 7, 6, 7, 6, 7),
)
KEYS, VALUES, BOTH = (0,), (1,), (0, 1)
WORK = (
    (14, BOTH, 0, {4: 1, 7: 1}),
    (19, BOTH, 1, {4: 1, 7: 1}),
    (23, KEYS, 2, {5: 1}),
    (0, KEYS, 3, {1: 1, 5: 1}),
    (28, VALUES, 2, {}),
    (28, VALUES, 3, {}),
)


def split(chunk):
    return chunk % UNITS, chunk // UNITS


def ring_order(way):
    seen = [0] * 2 * UNITS
    order = []
    for chunk in ORDERS[way]:
        order.append((*split(chunk), seen[chunk]))
        seen[chunk] += 1
    return order, seen


def body(
    pat_ref, res_ref, q_ref, k_ref, v_ref, sum_ref, car_ref,
    kb0, kb1, kb2, kb3, vb0, vb1, vb2, vb3, qb0, qb1, qb2, qb3, ob0, ob1,
    pb2, pb3, ksel, vsel, diag, pats,
    kx_send, kx_recv, own_sem, z_send, z_recv, e_send, e_recv, q_send, q_recv, o_send, o_recv, o_own,
    pat_sem, car_send, car_recv,
):
    kv = ((kb0, kb1, kb2, kb3), (vb0, vb1, vb2, vb3))
    kv_in = (k_ref, v_ref)
    qb = (qb0, qb1, qb2, qb3)
    ob = (ob0, ob1)
    pb = {2: pb2, 3: pb3}
    seg = lax.axis_index("segment")
    me = lax.axis_index("seq")
    z = me // NX
    x = lax.rem(me, NX)
    nseg = lax.axis_size("segment")

    def at_x(d):
        return (seg, z * NX + lax.rem(x + d, NX))

    def at_z(d):
        return (seg, lax.rem(z + d + NZ, NZ) * NX + x)

    after = (lax.rem(seg + 1, nseg), me)
    before = (lax.rem(seg + nseg - 1, nseg), me)

    def pat_copy(u):
        return pltpu.make_async_copy(
            pat_ref.at[0, u % 2, 2 * x + u // 2], pats.at[u], pat_sem.at[u]
        )

    def kv_src(u, t, who):
        cols = pl.multiple_of((2 * who + u // 2) * HD, HD)
        return kv_in[t].at[0, u % 2, :, pl.ds(cols, HD)]

    def q_src(u, who):
        cols = pl.multiple_of((2 * who + u // 2) * WIDE, WIDE)
        return q_ref.at[0, u % 2, :, pl.ds(cols, WIDE)]

    def own_copy(u, t):
        return pltpu.make_async_copy(
            kv_src(u, t, x), kv[t][u].at[z * NX + x], own_sem.at[u, t]
        )

    def own_q(u):
        return pltpu.make_async_copy(q_src(u, x), qb[u].at[x], q_recv.at[u, NX - 1])

    barrier = pltpu.get_barrier_semaphore()
    peers = [at_x(1), at_x(2), at_x(3), at_z(1), at_z(-1), after, before]
    for peer in peers:
        pl.semaphore_signal(barrier, inc=1, device_id=peer, device_id_type=MESH)
    for u in range(UNITS):
        for t in (0, 1):
            own_copy(u, t).start()
    for u in range(UNITS):
        pat_copy(u).start()
        own_q(u).start()
    row = lax.broadcasted_iota(jnp.int32, (BLOCK, BLOCK), 0)
    col = lax.broadcasted_iota(jnp.int32, (BLOCK, BLOCK), 1)
    diag[...] = jnp.where(row >= col, 0.0, NEG).astype(jnp.float32)
    vsel[:, pl.ds(HD, HD)] = jnp.ones((NSEL * BLOCK, HD), jnp.bfloat16)
    pl.semaphore_wait(barrier, len(peers))

    def kx_copy(u, t, d):
        to = lax.rem(x + d, NX)
        return pltpu.make_async_remote_copy(
            src_ref=kv_src(u, t, to),
            dst_ref=kv[t][u].at[z * NX + x],
            send_sem=kx_send.at[u, t, d - 1],
            recv_sem=kx_recv.at[u, t, d - 1],
            device_id=at_x(d),
            device_id_type=MESH,
        )

    def kx_arrived(u, t, d):
        frm = lax.rem(x + NX - d, NX)
        slot = kv[t][u].at[z * NX + frm]
        pltpu.make_async_copy(slot, slot, kx_recv.at[u, t, d - 1]).wait()

    def q_copy(u, d):
        to = lax.rem(x + d, NX)
        return pltpu.make_async_remote_copy(
            src_ref=q_src(u, to),
            dst_ref=qb[u].at[x],
            send_sem=q_send.at[u, d - 1],
            recv_sem=q_recv.at[u, d - 1],
            device_id=at_x(d),
            device_id_type=MESH,
        )

    carry = pltpu.make_async_remote_copy(
        src_ref=res_ref.at[0],
        dst_ref=car_ref,
        send_sem=car_send,
        recv_sem=car_recv,
        device_id=after,
        device_id_type=MESH,
    )
    chunks = [split(chunk) for chunk in CHUNKS]
    early = [split(chunk) for chunk in EARLY]

    def early_copy(way, u, t, d):
        part = kv[t][u].at[z * NX + lax.rem(x + NX - d, NX)]
        return pltpu.make_async_remote_copy(
            src_ref=part,
            dst_ref=part,
            send_sem=e_send.at[way, u, t, d],
            recv_sem=e_recv.at[way, u, t, d],
            device_id=at_z(1 if way == 0 else -1),
            device_id_type=MESH,
        )

    def early_arrived(way, u, t, d):
        origin = lax.rem(z + (NZ - 1 if way == 0 else 1), NZ)
        part = kv[t][u].at[origin * NX + lax.rem(x + NX - d, NX)]
        pltpu.make_async_copy(part, part, e_recv.at[way, u, t, d]).wait()


    def rows(u, t, origin):
        return kv[t][u].at[pl.ds(lax.rem(origin + NZ, NZ) * NX, NX)]

    def z_copy(way, u, t, step):
        sign = 1 if way == 0 else -1
        part = rows(u, t, z - sign * step)
        return pltpu.make_async_remote_copy(
            src_ref=part,
            dst_ref=part,
            send_sem=z_send.at[way, u, t, step],
            recv_sem=z_recv.at[way, u, t, step],
            device_id=at_z(sign),
            device_id_type=MESH,
        )

    def z_arrived(way, u, t, step):
        if step == 0 and (u, t) in early:
            for d in range(NX):
                early_arrived(way, u, t, d)
            return
        sign = 1 if way == 0 else -1
        part = rows(u, t, z - sign * (step + 1))
        pltpu.make_async_copy(part, part, z_recv.at[way, u, t, step]).wait()

    orders = [ring_order(0), ring_order(1)]
    places = len(orders[0][0])

    def hops(way, u, t):
        return orders[way][1][t * UNITS + u]

    def sends(way, u, t, step):
        if way == 0:
            return jnp.logical_and(z >= step, z < NZ - 1)
        return lax.rem(z + step, NZ) < hops(way, u, t)

    def receives(way, u, t, step):
        if way == 0:
            return z > step
        return lax.rem(z + 1 + step, NZ) < hops(way, u, t)

    opens = {}
    for p in range(places):
        for way in (0, 1):
            u, t, step = orders[way][0][p]
            opens.setdefault((u, t), (p, way))

    for u, t in chunks:
        for d in (1, 2, 3):
            kx_copy(u, t, d).start()
        if (u, t) in early:
            own_copy(u, t).wait()
            for way in (0, 1):

                @pl.when(sends(way, u, t, 0))
                def _():
                    early_copy(way, u, t, 0).start()

    carry.start()
    for u in range(UNITS):
        for d in (2, 1, 3):
            q_copy(u, d).start()

    def place_step(p):
        for way in (0, 1):
            u, t, step = orders[way][0][p]
            if step == 0:
                if opens[u, t] == (p, way):
                    if (u, t) not in early:
                        own_copy(u, t).wait()
                    for d in (1, 2, 3):
                        kx_arrived(u, t, d)

            @pl.when(sends(way, u, t, step))
            def _():
                if step:
                    z_arrived(way, u, t, step - 1)
                if step == 0 and (u, t) in early:
                    for d in (1, 2, 3):
                        early_copy(way, u, t, d).start()
                else:
                    z_copy(way, u, t, step).start()

    def whole(u, t):
        for way in (0, 1):
            for step in range(hops(way, u, t)):
                ends = receives(way, u, t, step)
                if step + 1 < hops(way, u, t):
                    ends = jnp.logical_and(ends, jnp.logical_not(sends(way, u, t, step + 1)))

                @pl.when(ends)
                def _():
                    z_arrived(way, u, t, step)

    def picks(u, b):
        return [pats[u, m, z * NX + b] for m in range(NSEL)]

    def take_keys(u, chosen):
        bias = []
        for m, pick in enumerate(chosen):
            ksel[pl.ds(m * BLOCK, BLOCK), :] = kv[0][u][jnp.maximum(pick, 0)]
            bias.append(jnp.where(pick >= 0, 0.0, NEG).astype(jnp.float32))
        return bias

    def take_values(u, chosen):
        for m, pick in enumerate(chosen):
            vsel[pl.ds(m * BLOCK, BLOCK), pl.ds(0, HD)] = kv[1][u][jnp.maximum(pick, 0)]

    def weigh(u, b, h, bias):
        scores = lax.dot_general(
            qb[u].at[b][:, pl.ds(h * HD, HD)], ksel[...], (((1,), (1,)), ((), ())),
            preferred_element_type=jnp.float32,
        )
        parts = []
        for m in range(NSEL):
            part = scores[:, m * BLOCK : (m + 1) * BLOCK]
            parts.append(part + (diag[...] if m == 0 else bias[m]))
        top = parts[0]
        for part in parts[1:]:
            top = jnp.maximum(top, part)
        top = jnp.max(top, axis=1, keepdims=True)
        return jnp.concatenate(
            [jnp.exp2((part - top) * EXP2_SCALE).astype(jnp.bfloat16) for part in parts],
            axis=1,
        )

    def mix(u, b, h, weights):
        out = ob[u // 2].at[b]
        mixed = jnp.dot(weights, vsel[...], preferred_element_type=jnp.float32)
        mixed = (mixed[:, :HD] / mixed[:, HD:]).astype(jnp.bfloat16)
        for n in range(weights.shape[0] // BLOCK):
            cols = pl.ds((h + n) * HD, HD)
            one = mixed[n * BLOCK : (n + 1) * BLOCK]
            if u % 2:
                one = (out[:, cols].astype(jnp.float32) + one.astype(jnp.float32)).astype(
                    jnp.bfloat16
                )
            out[:, cols] = one

    def out_slot(cc, who):
        cols = pl.multiple_of((2 * who + cc) * WIDE, WIDE)
        return sum_ref.at[:, pl.ds(cols, WIDE)]

    def out_copy(cc, j, k):
        b = lax.rem(x + j, NX)
        return pltpu.make_async_remote_copy(
            src_ref=ob[cc].at[b],
            dst_ref=out_slot(cc, x),
            send_sem=o_send.at[cc, k],
            recv_sem=o_recv.at[cc, k],
            device_id=(seg, z * NX + b),
            device_id_type=MESH,
        )

    def out_own(cc):
        return pltpu.make_async_copy(ob[cc].at[x], out_slot(cc, x), o_own.at[cc])

    def away(k):
        return NX - 1 - k - jnp.where(k == 0, 1, 0) + jnp.where(k == 1, 1, 0)

    def blocks(run, steps):
        def one(k, _):
            b = lax.rem(x + away(k), NX)
            kept = None
            for half in (0, 1):
                for kk in range(NX):
                    due = steps.get((kk, half), ())
                    if due:

                        @pl.when(k == kk)
                        def _():
                            for p in due:
                                place_step(p)

                kept = run(k, b, half, kept)
            return 0

        lax.fori_loop(0, NX, one, 0)

    def arrived_q(u, b, k):
        slot = qb[u].at[b]
        pltpu.make_async_copy(slot, slot, q_recv.at[u, NX - 1 - away(k)]).wait()

    half_heads = GROUP // 2

    def send_before(cc, k):
        @pl.when(k >= 1)
        def _():
            out_copy(cc, away(k - 1), NX - 1 - away(k - 1)).start()

    def run_both(u):
        def run(k, b, half, kept):
            if half == 0:
                arrived_q(u, b, k)
                chosen = picks(u, b)
                kept = take_keys(u, chosen)
                take_values(u, chosen)
            for h in range(half * half_heads, (half + 1) * half_heads):
                mix(u, b, h, weigh(u, b, h, kept))
            if half == 1 and u % 2 == 1:
                send_before(u // 2, k)
            return kept

        return run

    def run_weights(u):
        def run(k, b, half, kept):
            if half == 0:
                arrived_q(u, b, k)
                kept = take_keys(u, picks(u, b))
            for h in range(half * half_heads, (half + 1) * half_heads):
                pb[u][b, pl.ds(h * BLOCK, BLOCK), :] = weigh(u, b, h, kept)
            return kept

        return run

    def run_values(u):
        def run(k, b, half, kept):
            if half == 0:
                take_values(u, picks(u, b))
            for h in range(half * half_heads, (half + 1) * half_heads, TOGETHER):
                mix(u, b, h, pb[u][b, pl.ds(h * BLOCK, TOGETHER * BLOCK), :])
            if half == 1 and u % 2 == 1:
                send_before(u // 2, k)
            return kept

        return run

    done = 0

    def catch_up(to):
        nonlocal done
        while done < min(to, places):
            place_step(done)
            done += 1

    for u in range(UNITS):
        pat_copy(u).wait()
    runs = {KEYS: run_weights, VALUES: run_values, BOTH: run_both}
    for before, kinds, u, pauses in WORK:
        catch_up(before)
        for kind in kinds:
            whole(u, kind)
        steps = {}
        for at, count in pauses.items():
            steps[divmod(at, 2)] = range(done, done + count)
            done += count
        blocks(runs[kinds](u), steps)
        if u % 2 and kinds != KEYS:
            out_own(u // 2).start()

    for cc in (0, 1):
        for k in range(NX - 1):
            slot = out_slot(cc, lax.rem(x + 1 + k, NX))
            pltpu.make_async_copy(slot, slot, o_recv.at[cc, k]).wait()
            out_copy(cc, NX - 1 - k, k).wait_send()
        out_own(cc).wait()
    carry.wait()
    for u in range(UNITS):
        for d in (1, 2, 3):
            q_copy(u, d).wait_send()
            for t in (0, 1):
                kx_copy(u, t, d).wait_send()
    for way in (0, 1):
        for u, t, step in orders[way][0]:

            @pl.when(sends(way, u, t, step))
            def _():
                if step == 0 and (u, t) in early:
                    for d in range(NX):
                        early_copy(way, u, t, d).wait_send()
                else:
                    z_copy(way, u, t, step).wait_send()


def local(residual, query_rows, key_rows, value_rows, pattern):
    tokens, width = residual.shape[1:]
    any_spec = pl.BlockSpec(memory_space=pl.ANY)
    dma = pltpu.SemaphoreType.DMA
    bf16 = jnp.bfloat16
    layer_sum, carried = pl.pallas_call(
        body,
        name="relay_attention",
        out_shape=[pltpu.VMEM((tokens, width), bf16)] * 2,
        in_specs=[any_spec] * 5,
        out_specs=[pl.BlockSpec(memory_space=pltpu.VMEM)] * 2,
        scratch_shapes=[pltpu.VMEM((NZ * NX, BLOCK, HD), bf16)] * 8
        + [pltpu.VMEM((NX, BLOCK, WIDE), bf16)] * 6
        + [pltpu.VMEM((NX, GROUP * BLOCK, NSEL * BLOCK), bf16)] * 2
        + [
            pltpu.VMEM((NSEL * BLOCK, HD), bf16),
            pltpu.VMEM((NSEL * BLOCK, 2 * HD), bf16),
            pltpu.VMEM((BLOCK, BLOCK), jnp.float32),
            pltpu.SMEM((UNITS, NSEL, NZ * NX), jnp.int32),
            dma((UNITS, 2, 3)), dma((UNITS, 2, 3)), dma((UNITS, 2)),
            dma((2, UNITS, 2, 4)), dma((2, UNITS, 2, 4)),
            dma((2, UNITS, 2, NX)), dma((2, UNITS, 2, NX)),
            dma((UNITS, 3)), dma((UNITS, 4)),
            dma((2, 3)), dma((2, 3)), dma((2,)),
            dma((UNITS,)), dma(()), dma(()),
        ],
        compiler_params=pltpu.CompilerParams(
            collective_id=0, has_side_effects=True, vmem_limit_bytes=58 * 2**20
        ),
    )(jnp.swapaxes(pattern, 3, 4), residual, query_rows, key_rows, value_rows)
    out = carried.astype(jnp.float32) + layer_sum.astype(jnp.float32)
    return out[None]


def solution(mesh):
    return jax.shard_map(
        local,
        mesh=mesh,
        in_specs=(
            P("segment", "seq", None),
            P("segment", None, "seq", None),
            P("segment", None, "seq", None),
            P("segment", None, "seq", None),
            P("segment", None, None, None, None),
        ),
        out_specs=P("segment", "seq", None),
        check_vma=False,
    )
```
